32 devices in a mesh: section: 2 (over core), rep: 4 (over z), expert: 4 (over y, x).
Axes of the slice: x: 2, y: 2, z: 4, core: 2. Of those that a mesh axis runs over, the one named last changes fastest.
Arguments:
- activations: bfloat16 [2, 4, 256, 7168], P('section', 'rep', 'expert'), may hold values from -6 to 6
- routes: int32 [2, 4, 256, 8], P('section', 'rep', 'expert'), may hold values from 0 to 255, all different within a row; in each aligned block of 64 rows (0 to 63, 64 to 127, ..., all dimensions but the last counted through in order) at most 2 rows name the same one
- gate_values: float32 [2, 4, 256, 8], P('section', 'rep', 'expert'), may hold values from 0.1 to 1
- w_gate: bfloat16 [2, 7168, 8192], P('section', None, 'expert'), may hold values from -0.0625 to 0.0625
- w_up: bfloat16 [2, 7168, 8192], P('section', None, 'expert'), may hold values from -0.0625 to 0.0625
- w_down: bfloat16 [2, 8192, 7168], P('section', 'expert'), may hold values from -0.125 to 0.125
Outputs:
- handed: bfloat16 [2, 4, 256, 7168], P('section', 'rep', 'expert')
- load_share: float32 [2, 4], P('section')
The draws below stay inside these ranges and needn't reach their ends.
Inputs may be any that keep to these rules, and one draw needn't show every extreme that they name: The 8 routes of a token name different experts; in each aligned block of 64 tokens (the tokens of one device) at most 2 tokens name one expert.
All inputs are finite; a program needn't handle non-finite values.
Results may differ from the reference program's by a relative error of at most 0.012.
Values may be sent and summed in bfloat16 or wider, within the bound.
No kernel may reach another device: no remote copies, remote signals or barrier semaphores. Data moves between devices by JAX's collectives and lax.ppermute only.
A program may use at most 128 MiB of HBM per device.

```python
import math
import jax
import jax.numpy as jnp
import numpy as np
from jax import lax

D = 7168
HIDDEN_SIZE = 2048
ALL_EXPERTS = 256
TOP = 8
EXPERTS = 4
CAPACITY = 2
TOK_DEV = 64
TOKENS = 256
SECTIONS = 2
REPS = 4
N_EXPERT = 4


def shard_levels(stream_key, shape, split, low, top_value):
    loudness, own = 1.0, jax.random.fold_in(stream_key, 6)
    for axis_at, shards_of in split:
        steps = jnp.exp(jax.random.uniform(jax.random.fold_in(own, axis_at), (shards_of,), jnp.float32, low / len(split), top_value / len(split)))
        loudness = loudness * jnp.repeat(steps, shape[axis_at] // shards_of).reshape([-1 if axis == axis_at else 1 for axis in range(len(shape))])
    return loudness


def deal_out(stream_key, own, number, rows, count, top, limit, lean):
    sequence = jax.random.permutation(stream_key, count)
    crowded, common = shares(count, rows * top, limit, lean, True), shares(count, rows * top, limit, lean, False)
    places = jnp.arange(count)

    def named(sizes, rotation):
        used = int((sizes > 0).sum())
        fixed = max(1, used // 4)
        moved = fixed + (places - fixed + rotation * (used - fixed)) % max(1, count - fixed)
        return jnp.zeros((count,), jnp.int32).at[sequence[jnp.where(places < fixed, places, moved)]].set(jnp.asarray(sizes, jnp.int32))

    sizes = jnp.where(number % 4 == 0, named(crowded, number // 4), named(common, number - number // 4 - 1))
    mixed = jax.random.permutation(jax.random.fold_in(own, 3), count)
    donor, taker = mixed[0:count // 2 * 2:2], mixed[1:count // 2 * 2:2]
    room = jnp.minimum(sizes[donor] - 1, limit - sizes[taker]) // 2
    room = jnp.where((donor == sequence[0]) | (taker == sequence[0]) | (sizes[taker] == 0), 0, jnp.maximum(room, 0))
    moved = jax.random.randint(jax.random.fold_in(own, 4), (count // 2,), 0, 1 << 20) % (room + 1)
    sizes = sizes.at[donor].add(-moved).at[taker].add(moved)
    items = jnp.searchsorted(jnp.cumsum(sizes), jnp.arange(rows * top), side="right").astype(jnp.int32)
    grid = items.reshape(top, rows).T
    grid = grid[jax.random.permutation(jax.random.fold_in(own, 1), rows)]
    rotation = jax.random.randint(jax.random.fold_in(own, 2), (rows, 1), 0, top)
    return jnp.take_along_axis(grid, (jnp.arange(top)[None, :] + rotation) % top, axis=1)


def shares(number_of, total, most, skew, full):
    weights = [(1 << 20) // math.isqrt(grade ** skew) + 1 for grade in range(1, number_of + 1)]
    largest = most if full else min(most, max(-(-total // number_of), total * weights[0] // sum(weights)))
    least = 1 if total - largest >= number_of - 1 else 0
    given, surplus = [largest] + [least] * (number_of - 1), total - largest - least * (number_of - 1)
    while surplus > 0:
        candidates = [i for i in range(1, number_of) if given[i] < largest] or [i for i in range(1, number_of) if given[i] < most]
        whole, budget = sum([weights[i] for i in candidates]), surplus
        for i in candidates:
            extra = min(most - given[i], max(1, budget * weights[i] // whole), surplus)
            given[i] = given[i] + extra
            surplus = surplus - extra
    return np.array(given)


def noise(own_key, dims, width, bound, shards=(), kind=jnp.bfloat16):
    loudness = shard_levels(own_key, dims, shards, -0.22, 0.18) if shards else 1.0
    array = jax.random.normal(own_key, dims, jnp.float32) * width * loudness
    return jnp.minimum(jnp.maximum(array, -bound), bound).astype(kind)


def setup_inputs(seed: int = 0) -> dict:
    seeds = jax.random.split(jax.random.key(seed), 7)
    activations = noise(seeds[0], (SECTIONS, REPS, TOKENS, D), 1.0, 6.0, ((0, 2), (1, 4), (2, 4)))
    routes_keys = jax.random.split(jax.random.fold_in(seeds[1], 1), SECTIONS * REPS * TOKENS // TOK_DEV)
    routes_turns = jax.random.permutation(jax.random.fold_in(seeds[1], 3), SECTIONS * REPS * TOKENS // TOK_DEV)
    routes = jax.vmap(lambda own, number: deal_out(jax.random.fold_in(seeds[1], 2), own, number, TOK_DEV, ALL_EXPERTS, TOP, CAPACITY, 2))(routes_keys, routes_turns).reshape((SECTIONS, REPS, TOKENS, TOP))
    gate_values = jnp.clip(jnp.exp(math.log(1.0) - 2.3025851 * jax.random.uniform(seeds[2], (SECTIONS, REPS, TOKENS, TOP), jnp.float32) ** shard_levels(seeds[2], (SECTIONS, REPS, TOKENS, TOP), ((0, 2), (1, 4), (2, 4)), -0.2, 0.2)), 0.1, 1.0)
    w_gate = noise(seeds[3], (SECTIONS, D, EXPERTS * HIDDEN_SIZE), D ** -0.5, 0.0625, ((0, 2), (2, 4)))
    w_up = noise(seeds[4], (SECTIONS, D, EXPERTS * HIDDEN_SIZE), D ** -0.5, 0.0625, ((0, 2), (2, 4)))
    w_down = noise(seeds[5], (SECTIONS, EXPERTS * HIDDEN_SIZE, D), HIDDEN_SIZE ** -0.5, 0.125, ((0, 2), (1, 4)))
    return {"activations": activations, "routes": routes, "gate_values": gate_values, "w_gate": w_gate, "w_up": w_up, "w_down": w_down}


def route_tables(route_ids, gates):
    expert_ids = jnp.arange(EXPERTS, dtype=jnp.int32)
    matches = (route_ids[:, :, None] == expert_ids[None, None, :]).astype(jnp.float32)
    hits = jnp.sum(matches, axis=1)
    mass = jnp.sum(gates.astype(jnp.float32)[:, :, None] * matches, axis=1)
    return hits, mass


def slot_picks(hits):
    before = jnp.cumsum(hits, axis=0) - hits
    slots = jnp.arange(CAPACITY).astype(jnp.float32)
    picks = hits[:, :, None] * (before[:, :, None] == slots[None, None, :]).astype(jnp.float32)
    return jnp.transpose(picks, (1, 2, 0))


def span_mix(acts, route_ids, gates, w_gate, w_up, w_down):
    tok_dev = acts.shape[0] // N_EXPERT
    members = N_EXPERT // EXPERTS
    slice_width = HIDDEN_SIZE // members
    highest = lax.Precision.HIGHEST
    hits, mass = route_tables(route_ids, gates)
    weights_b = mass.astype(jnp.bfloat16)
    picks = jax.vmap(slot_picks)(hits.reshape(N_EXPERT, tok_dev, EXPERTS))
    acts_blocks = acts.reshape(N_EXPERT, tok_dev, D).astype(jnp.float32)
    rows = jnp.einsum("bect,btd->ebcd", picks, acts_blocks, precision=highest).astype(jnp.bfloat16)
    rows = rows.reshape(EXPERTS, N_EXPERT * CAPACITY, D)
    weight_blocks = weights_b.reshape(N_EXPERT, tok_dev, EXPERTS).astype(jnp.float32)
    row_weights = jnp.einsum("bect,bte->ebc", picks, weight_blocks, precision=highest)
    row_weights = row_weights.reshape(EXPERTS, N_EXPERT * CAPACITY)

    def add_slice(slice_index, running):
        slice_index = jnp.asarray(slice_index).astype(jnp.int32)
        expert_now = (slice_index // members).astype(jnp.int32)
        begin = (slice_index * slice_width).astype(jnp.int32)
        rows_now = lax.dynamic_index_in_dim(rows, expert_now, 0, keepdims=False)
        weight_now = lax.dynamic_index_in_dim(row_weights, expert_now, 0, keepdims=False)
        gate_cols = lax.dynamic_slice_in_dim(w_gate, begin, slice_width, 1)
        up_cols = lax.dynamic_slice_in_dim(w_up, begin, slice_width, 1)
        down_rows = lax.dynamic_slice_in_dim(w_down, begin, slice_width, 0)
        gate_proj = jnp.dot(rows_now, gate_cols, preferred_element_type=jnp.float32)
        up_proj = jnp.dot(rows_now, up_cols, preferred_element_type=jnp.float32)
        hidden = (jax.nn.silu(gate_proj) * up_proj).astype(jnp.bfloat16)
        partial_out = jnp.dot(hidden, down_rows, preferred_element_type=jnp.float32)
        weighted = (weight_now[:, None] * partial_out).astype(jnp.bfloat16)
        weighted = lax.optimization_barrier(weighted)
        return running.at[expert_now].add(weighted.astype(jnp.float32))

    start_sum = jnp.zeros((EXPERTS, N_EXPERT * CAPACITY, D), jnp.float32)
    running = lax.fori_loop(0, N_EXPERT, add_slice, start_sum)
    running = running.reshape(EXPERTS, N_EXPERT, CAPACITY, D)
    mixed = jnp.einsum("bect,ebcd->btd", picks, running, precision=highest)
    return mixed.reshape(N_EXPERT * tok_dev, D).astype(jnp.bfloat16), jnp.sum(mass, axis=0)


def reference(activations, routes, gate_values, w_gate, w_up, w_down):
    def per_section(section_args):
        acts_section, routes_section, gates_section, gate_w, up_w, down_w = section_args

        def per_span(span_args):
            acts_span, routes_span, gates_span = span_args
            return span_mix(acts_span, routes_span, gates_span, gate_w, up_w, down_w)

        mixed_all, mass_all = lax.map(per_span, (acts_section, routes_section, gates_section))
        return mixed_all, jnp.sum(mass_all, axis=0)

    mixed, mass = lax.map(per_section, (activations, routes, gate_values, w_gate, w_up, w_down))
    handed = jnp.roll(mixed, 1, axis=0)
    load_share = mass / jnp.float32(REPS * TOKENS)
    return handed, load_share
```

```python
import functools

import jax
import jax.numpy as jnp
from jax import lax
from jax.experimental import pallas as pl
from jax.experimental.pallas import tpu as pltpu
from jax.sharding import PartitionSpec as P

EXPERTS = 4
CAPACITY = 2
BF16 = jnp.bfloat16
F32 = jnp.float32
ANY = pl.BlockSpec(memory_space=pl.ANY)
VMEM = pl.BlockSpec(memory_space=pltpu.VMEM)
SMEM = pl.BlockSpec(memory_space=pltpu.SMEM)


def partner(index, distance, count):
    if count & (count - 1) == 0:
        return index ^ distance
    return (index + distance) % count


def largest_chunk(total, limit, unit):
    best = unit
    for size in range(unit, min(total, limit) + 1, unit):
        if total % size == 0:
            best = size
    return best


def route_kernel(peers, members, me_ref, routes_ref, gates_ref, acts_ref, *refs):
    row_refs, picks_ref, mass_ref = refs[:peers], refs[peers], refs[peers + 1]
    me = me_ref[0]
    routes = routes_ref[...]
    gates = gates_ref[...]
    tokens = routes.shape[1]
    hits, mass = [], []
    for expert in range(EXPERTS):
        match = routes == expert
        hits.append(jnp.sum(jnp.where(match, 1.0, 0.0), axis=0, keepdims=True))
        mass.append(jnp.sum(jnp.where(match, gates, 0.0), axis=0, keepdims=True))
    hits = jnp.concatenate(hits, axis=0)
    mass = jnp.concatenate(mass, axis=0)
    mass_ref[...] = jnp.broadcast_to(jnp.sum(mass, axis=1, keepdims=True), mass_ref.shape)
    earlier = lax.broadcasted_iota(jnp.int32, (tokens, tokens), 0) < lax.broadcasted_iota(
        jnp.int32, (tokens, tokens), 1
    )
    before = jnp.dot(hits, jnp.where(earlier, 1.0, 0.0), preferred_element_type=F32)
    weights = mass.astype(BF16).astype(F32)
    picks, scaled = [], []
    for distance in range(peers):
        expert = partner(me, distance, peers) // members
        chosen = lax.broadcasted_iota(jnp.int32, hits.shape, 0) == expert
        hit = jnp.sum(jnp.where(chosen, hits, 0.0), axis=0, keepdims=True)
        seen = jnp.sum(jnp.where(chosen, before, 0.0), axis=0, keepdims=True)
        weight = jnp.sum(jnp.where(chosen, weights, 0.0), axis=0, keepdims=True)
        for slot in range(CAPACITY):
            pick = jnp.where(seen == slot, hit, 0.0)
            picks.append(pick)
            scaled.append(pick * weight)
    picks = jnp.concatenate(picks, axis=0)
    picks_ref[...] = jnp.concatenate(scaled, axis=0).astype(BF16)
    rows = jnp.dot(picks.astype(BF16), acts_ref[...], preferred_element_type=F32).astype(BF16)
    for distance in range(peers):
        row_refs[distance][...] = rows[distance * CAPACITY : (distance + 1) * CAPACITY]


def expert_kernel(peers, depth, span, slots, *refs):
    row_refs = refs[:peers]
    gate_ref, up_ref, down_ref = refs[peers : peers + 3]
    out_refs = refs[peers + 3 : 2 * peers + 3]
    gate_buf, up_buf, down_buf, rows_ref, gate_sem, up_sem, down_sem = refs[2 * peers + 3 :]
    width, hidden = gate_ref.shape
    steps, pieces = width // depth, width // span
    down_slots = down_buf.shape[0]

    def first(ref, buf, sem, step):
        return pltpu.make_async_copy(
            ref.at[pl.ds(step * depth, depth), :], buf.at[step % slots], sem.at[step % slots]
        )

    def second(piece):
        return pltpu.make_async_copy(
            down_ref.at[:, pl.ds(piece * span, span)],
            down_buf.at[piece % down_slots],
            down_sem.at[piece % down_slots],
        )

    for step in range(min(slots, steps)):
        first(gate_ref, gate_buf, gate_sem, step).start()
        first(up_ref, up_buf, up_sem, step).start()
    for piece in range(min(down_slots, pieces)):
        second(piece).start()
    rows_ref[...] = jnp.concatenate([ref[...].astype(F32) for ref in row_refs], axis=0).astype(BF16)
    rows = rows_ref.shape[0]
    gate = jnp.zeros((rows, hidden), F32)
    up = jnp.zeros((rows, hidden), F32)
    for step in range(steps):
        first(gate_ref, gate_buf, gate_sem, step).wait()
        first(up_ref, up_buf, up_sem, step).wait()
        part = rows_ref[:, step * depth : (step + 1) * depth]
        gate = gate + jnp.dot(part, gate_buf[step % slots], preferred_element_type=F32)
        up = up + jnp.dot(part, up_buf[step % slots], preferred_element_type=F32)
        if step + slots < steps:
            first(gate_ref, gate_buf, gate_sem, step + slots).start()
            first(up_ref, up_buf, up_sem, step + slots).start()
    inner = (gate / (1.0 + jnp.exp(-gate)) * up).astype(BF16)
    for piece in range(pieces):
        second(piece).wait()
        result = jnp.dot(inner, down_buf[piece % down_slots], preferred_element_type=F32)
        result = result.astype(BF16)
        for source in range(peers):
            out_refs[source][:, piece * span : (piece + 1) * span] = result[
                source * CAPACITY : (source + 1) * CAPACITY
            ]
        if piece + down_slots < pieces:
            second(piece + down_slots).start()


def combine_kernel(peers, picks_ref, *refs):
    row_refs, out_ref = refs[:peers], refs[peers]
    rows = jnp.concatenate([ref[...].astype(F32) for ref in row_refs], axis=0).astype(BF16)
    out_ref[...] = lax.dot_general(
        picks_ref[...], rows, (((0,), (0,)), ((), ())), preferred_element_type=F32
    ).astype(BF16)


def local(activations, routes, gate_values, w_gate, w_up, w_down):
    peers = lax.axis_size("expert")
    sections = lax.axis_size("section")
    reps = lax.axis_size("rep")
    members = peers // EXPERTS
    tokens, width = activations.shape[2:]
    hidden = w_gate.shape[2]
    me = lax.axis_index("expert").astype(jnp.int32).reshape(1)
    rows_shape = jax.ShapeDtypeStruct((CAPACITY, width), BF16)
    *sent, picks, mass = pl.pallas_call(
        functools.partial(route_kernel, peers, members),
        out_shape=[rows_shape] * peers
        + [
            jax.ShapeDtypeStruct((peers * CAPACITY, tokens), BF16),
            jax.ShapeDtypeStruct((EXPERTS, 128), F32),
        ],
        in_specs=[SMEM, VMEM, VMEM, VMEM],
        out_specs=[VMEM] * (peers + 2),
        compiler_params=pltpu.CompilerParams(vmem_limit_bytes=8 << 20),
        name="route",
    )(me, routes[0, 0].T, gate_values[0, 0].T, activations[0, 0])

    order = sorted(range(1, peers), key=lambda d: -bin(d).count("1"))
    got = [sent[0]] + [None] * (peers - 1)
    for distance in order:
        route = [(i, partner(i, distance, peers)) for i in range(peers)]
        got[distance] = lax.ppermute(sent[distance], "expert", route)
    onward = [(s, (s + 1) % sections) for s in range(sections)]
    picks = lax.ppermute(picks, "section", onward)

    total = mass[:, :1]
    for axis, count in (("expert", peers), ("rep", reps)):
        reach = 1
        while reach < count:
            route = [(i, i ^ reach) for i in range(count)]
            total = total + lax.ppermute(total, axis, route)
            reach *= 2

    depth = largest_chunk(width, 512, 128)
    span = largest_chunk(width, 512, 128)
    back = pl.pallas_call(
        functools.partial(expert_kernel, peers, depth, span, 4),
        out_shape=[rows_shape] * peers,
        in_specs=[VMEM] * peers + [ANY] * 3,
        out_specs=[VMEM] * peers,
        scratch_shapes=[
            pltpu.VMEM((4, depth, hidden), BF16),
            pltpu.VMEM((4, depth, hidden), BF16),
            pltpu.VMEM((4, hidden, span), BF16),
            pltpu.VMEM((peers * CAPACITY, width), BF16),
            pltpu.SemaphoreType.DMA((4,)),
            pltpu.SemaphoreType.DMA((4,)),
            pltpu.SemaphoreType.DMA((4,)),
        ],
        compiler_params=pltpu.CompilerParams(vmem_limit_bytes=40 << 20),
        name="expert",
    )(*got, w_gate[0], w_up[0], w_down[0])

    home = [None] * peers
    for distance in order + [0]:
        route = [
            (s * peers + partner(i, distance, peers), (s + 1) % sections * peers + i)
            for s in range(sections)
            for i in range(peers)
        ]
        home[distance] = lax.ppermute(back[distance], ("section", "expert"), route)
    handed = pl.pallas_call(
        functools.partial(combine_kernel, peers),
        out_shape=jax.ShapeDtypeStruct((tokens, width), BF16),
        in_specs=[VMEM] * (peers + 1),
        out_specs=VMEM,
        compiler_params=pltpu.CompilerParams(vmem_limit_bytes=16 << 20),
        name="combine",
    )(picks, *home)
    load_share = total[:, 0] / F32(reps * peers * tokens)
    return (handed[None, None], load_share[None])


def solution(mesh):
    placed = (
        P("section", "rep", "expert", None),
        P("section", "rep", "expert", None),
        P("section", "rep", "expert", None),
        P("section", None, "expert"),
        P("section", None, "expert"),
        P("section", "expert", None),
    )
    return jax.shard_map(
        local,
        mesh=mesh,
        in_specs=placed,
        out_specs=(P("section", "rep", "expert", None), P("section", None)),
        check_vma=False,
    )
```
